128 devices in a mesh: dp: 8 (over z_lo, x), expert: 16 (over z_hi, y, core).
Axes of the slice: x: 4, y: 4, z: 4 (z_hi: 2, z_lo: 2; z = z_hi * 2 + z_lo), core: 2. Of those that a mesh axis runs over, the one named last changes fastest.
Arguments:
- tokens: bfloat16 [16384, 2048], P(('dp', 'expert')), may hold values from -6 to 6
- cotangent: bfloat16 [16384, 2048], P(('dp', 'expert')), may hold values from -6 to 6
- expert_ids: int32 [16384, 4], P(('dp', 'expert')), may hold values from 0 to 15, all different within a row; in each aligned block of 128 rows (0 to 127, 128 to 255, ...) at most 48 rows name the same one
- gate_probs: bfloat16 [16384, 4], P(('dp', 'expert')), may hold values from 0.049804688 to 0.5
- w_in: bfloat16 [16, 2048, 1536], P('expert', 'dp'), may hold values from -0.125 to 0.125
- w_out: bfloat16 [16, 768, 2048], P('expert', 'dp'), may hold values from -0.21875 to 0.21875
- mom_in: float32 [16, 2048, 1536], P('expert', 'dp'), may hold values from -12 to 12
- mom_out: float32 [16, 768, 2048], P('expert', 'dp'), may hold values from -12 to 12
Outputs:
- layer_out: bfloat16 [16384, 2048], P(('dp', 'expert'))
- tokens_grad: bfloat16 [16384, 2048], P(('dp', 'expert'))
- gate_grad: bfloat16 [16384, 4], P(('dp', 'expert'))
- w_in_new: bfloat16 [16, 2048, 1536], P('expert', 'dp')
- w_out_new: bfloat16 [16, 768, 2048], P('expert', 'dp')
- mom_in_new: float32 [16, 2048, 1536], P('expert', 'dp')
- mom_out_new: float32 [16, 768, 2048], P('expert', 'dp')
The draws below stay inside these ranges and needn't reach their ends.
Inputs may be any that keep to these rules, and one draw needn't show every extreme that they name: `expert_ids`: each row names 4 different experts. Among the 128 tokens of one device (aligned blocks of rows), no expert is named more than 48 times, a bound that some block reaches.
All inputs are finite; a program needn't handle non-finite values.
Results may differ from the reference program's by a relative error of at most 0.009.
Values may be sent and summed in bfloat16 or wider, within the bound.
No kernel may reach another device: no remote copies, remote signals or barrier semaphores. Data moves between devices by JAX's collectives and lax.ppermute only.
A program may use at most 128 MiB of HBM per device.

```python
import math
import jax
import jax.numpy as jnp
import numpy as np
from jax import lax

D = 2048
FF = 768
TOP = 4
TOK_DEV = 128
EXPERTS = 16
CAP = 48
SLOTS = 768
TOKENS = 16384
N_DP = 8
N_EXPERT = 16


def shard_levels(key, shape, pieces, smallest, largest):
    def one(axis_at, parts):
        steps = jax.random.uniform(jax.random.fold_in(jax.random.fold_in(key, 6), axis_at), (parts,), jnp.float32, smallest / len(pieces), largest / len(pieces))
        return jnp.repeat(jnp.exp(steps), shape[axis_at] // parts).reshape((-1,) + (1,) * (len(shape) - axis_at - 1))

    loudness = one(*pieces[0])
    for cut in pieces[1:]:
        loudness = loudness * one(*cut)
    return loudness


def routed_block(rng, own, number, rows, amount, top, reach, skew):
    order = jax.random.permutation(rng, amount)
    heavy_load, usual = load_shares(amount, rows * top, reach, skew, True), load_shares(amount, rows * top, reach, skew, False)
    places = jnp.arange(amount)

    def named(lengths, offset_by):
        used = int((lengths > 0).sum())
        fixed = max(1, used // 4)
        passed = fixed + (places - fixed + offset_by * (used - fixed)) % max(1, amount - fixed)
        return jnp.zeros((amount,), jnp.int32).at[order[jnp.where(places < fixed, places, passed)]].set(jnp.asarray(lengths, jnp.int32))

    lengths = jnp.where(number % 4 == 0, named(heavy_load, number // 4), named(usual, number - number // 4 - 1))
    mixed = jax.random.permutation(jax.random.fold_in(own, 3), amount)
    donor, taker = mixed[0:amount // 2 * 2:2], mixed[1:amount // 2 * 2:2]
    slack = jnp.minimum(lengths[donor] - 1, reach - lengths[taker]) // 2
    slack = jnp.where((donor == order[0]) | (taker == order[0]) | (lengths[taker] == 0), 0, jnp.maximum(slack, 0))
    passed = jax.random.randint(jax.random.fold_in(own, 4), (amount // 2,), 0, 1 << 20) % (slack + 1)
    lengths = lengths.at[donor].add(-passed).at[taker].add(passed)
    members = jnp.searchsorted(jnp.cumsum(lengths), jnp.arange(rows * top), side="right").astype(jnp.int32)
    grid = members.reshape(top, rows).T
    grid = grid[jax.random.permutation(jax.random.fold_in(own, 1), rows)]
    offset_by = jax.random.randint(jax.random.fold_in(own, 2), (rows, 1), 0, top)
    return jnp.take_along_axis(grid, (jnp.arange(top)[None, :] + offset_by) % top, axis=1)


def load_shares(amount, total, bound, lean, full):
    weights = [(1 << 20) // math.isqrt(grade ** lean) + 1 for grade in range(1, amount + 1)]
    largest = bound if full else min(bound, max(-(-total // amount), total * weights[0] // sum(weights)))
    least = 1 if total - largest >= amount - 1 else 0
    holding, spare = [largest] + [least] * (amount - 1), total - largest - least * (amount - 1)
    while spare > 0:
        candidates = [i for i in range(1, amount) if holding[i] < largest] or [i for i in range(1, amount) if holding[i] < bound]
        pool, budget = sum([weights[i] for i in candidates]), spare
        for i in candidates:
            addition = min(bound - holding[i], max(1, budget * weights[i] // pool), spare)
            holding[i] = holding[i] + addition
            spare = spare - addition
    return np.array(holding)


def bell_draw(own_key, extent, deviation, most, cuts=(), kind=jnp.bfloat16):
    drawn = deviation * jax.random.normal(own_key, extent, jnp.float32)
    if cuts:
        drawn = drawn * shard_levels(own_key, extent, cuts, -0.22, 0.18)
    return jnp.clip(drawn, -most, most).astype(kind)


def setup_inputs(seed: int = 0) -> dict:
    key_list = jax.random.split(jax.random.key(seed), 9)
    tokens = bell_draw(key_list[0], (TOKENS, D), 1.0, 6.0, ((0, 128),))
    cotangent = bell_draw(key_list[1], (TOKENS, D), 1.0, 6.0, ((0, 128),))
    expert_ids_keys = jax.random.split(jax.random.fold_in(key_list[2], 1), TOKENS // TOK_DEV)
    expert_ids_turns = jax.random.permutation(jax.random.fold_in(key_list[2], 3), TOKENS // TOK_DEV)
    expert_ids = jax.vmap(lambda own, number: routed_block(jax.random.fold_in(key_list[2], 2), own, number, TOK_DEV, EXPERTS, TOP, CAP, 2))(expert_ids_keys, expert_ids_turns).reshape((TOKENS, TOP))
    gate_probs = jnp.clip(0.049804688 + 0.4501953 * jax.random.uniform(key_list[3], (TOKENS, TOP), jnp.float32) ** shard_levels(key_list[3], (TOKENS, TOP), ((0, 128),), -0.2, 0.2), 0.049804688, 0.5).astype(jnp.bfloat16)
    w_in = bell_draw(key_list[4], (EXPERTS, D, 2 * FF), D ** -0.5, 0.125, ((0, 16), (1, 8)))
    w_out = bell_draw(key_list[5], (EXPERTS, FF, D), FF ** -0.5, 0.21875, ((0, 16), (1, 8)))
    mom_in = bell_draw(key_list[6], (EXPERTS, D, 2 * FF), 2.0, 12.0, ((0, 16), (1, 8)), jnp.float32)
    mom_out = bell_draw(key_list[7], (EXPERTS, FF, D), 2.0, 12.0, ((0, 16), (1, 8)), jnp.float32)
    return {"tokens": tokens, "cotangent": cotangent, "expert_ids": expert_ids, "gate_probs": gate_probs, "w_in": w_in, "w_out": w_out, "mom_in": mom_in, "mom_out": mom_out}


beta_one = 0.9
beta_two = 0.99
learn_rate = 0.02
decay_rate = 0.1

def expert_pass(inputs, cots, gates, weight_in, weight_out):
    pre = jnp.einsum('erd,edf->erf', inputs.astype(jnp.float32), weight_in.astype(jnp.float32))
    gate_part = pre[..., :FF]
    up_part = pre[..., FF:]
    sig_part = jax.nn.sigmoid(gate_part)
    activated = gate_part * sig_part
    hidden = (activated * up_part).astype(jnp.bfloat16)
    expert_out = jnp.einsum('erf,efd->erd', hidden.astype(jnp.float32), weight_out.astype(jnp.float32))
    gate_col = gates.astype(jnp.float32)[..., None]
    weighted = (gate_col * expert_out).astype(jnp.bfloat16)
    slot_gate = lax.optimization_barrier(jnp.sum(cots.astype(jnp.float32) * expert_out, axis=-1)).astype(jnp.bfloat16)
    out_grad = (gate_col * cots.astype(jnp.float32)).astype(jnp.bfloat16)
    hidden_grad = jnp.einsum('erd,efd->erf', out_grad.astype(jnp.float32), weight_out.astype(jnp.float32))
    slope = sig_part * (1.0 + gate_part * (1.0 - sig_part))
    pre_grad = jnp.concatenate([hidden_grad * up_part * slope, hidden_grad * activated], axis=-1).astype(jnp.bfloat16)
    slot_grad = jnp.einsum('erf,edf->erd', pre_grad.astype(jnp.float32), weight_in.astype(jnp.float32)).astype(jnp.bfloat16)
    part_in = jnp.einsum('erd,erf->edf', inputs.astype(jnp.float32), pre_grad.astype(jnp.float32)).astype(jnp.bfloat16)
    part_out = jnp.einsum('erf,erd->efd', hidden.astype(jnp.float32), out_grad.astype(jnp.float32)).astype(jnp.bfloat16)
    return (weighted, slot_gate, slot_grad, part_in, part_out)

def lion_update(weight, moment, grad):
    blend = beta_one * moment + (1.0 - beta_one) * grad
    direction = blend / jnp.sqrt(blend * blend + 1.0)
    wide = weight.astype(jnp.float32)
    new_weight = (wide - learn_rate * (direction + decay_rate * wide)).astype(jnp.bfloat16)
    new_moment = beta_two * moment + (1.0 - beta_two) * grad
    return (new_weight, new_moment)

def reference(tokens, cotangent, expert_ids, gate_probs, w_in, w_out, mom_in, mom_out):
    blocks = N_DP * N_EXPERT
    pairs = TOK_DEV * TOP
    replica_rows = N_EXPERT * TOK_DEV
    expert_rows = expert_ids.reshape(blocks, pairs)
    onehot = (expert_rows[:, :, None] == jnp.arange(EXPERTS, dtype=jnp.int32)[None, None, :]).astype(jnp.int32)
    position = lax.optimization_barrier(jnp.sum((jnp.cumsum(onehot, axis=1) - onehot) * onehot, axis=2))
    source = (jnp.arange(blocks, dtype=jnp.int32) % N_EXPERT)[:, None]
    slot_index = (expert_rows * SLOTS + source * CAP + position).astype(jnp.int32).reshape(N_DP, N_EXPERT * pairs)
    replica_tokens = tokens.reshape(N_DP, replica_rows, D)
    replica_cots = cotangent.reshape(N_DP, replica_rows, D)
    replica_gates = gate_probs.reshape(N_DP, N_EXPERT * pairs)
    owner_row = jnp.repeat(jnp.arange(replica_rows, dtype=jnp.int32), TOP)
    total = EXPERTS * SLOTS

    def replica(carry, item):
        slots, rows_in, rows_cot, gates = item
        inputs = jnp.zeros((total, D), rows_in.dtype).at[slots].set(rows_in[owner_row]).reshape(EXPERTS, SLOTS, D)
        cots = jnp.zeros((total, D), rows_cot.dtype).at[slots].set(rows_cot[owner_row]).reshape(EXPERTS, SLOTS, D)
        gate_buf = jnp.zeros((total,), gates.dtype).at[slots].set(gates).reshape(EXPERTS, SLOTS)
        weighted, slot_gate, slot_grad, part_in, part_out = expert_pass(inputs, cots, gate_buf, w_in, w_out)
        layer_rows = lax.optimization_barrier(jnp.sum(weighted.reshape(total, D)[slots].astype(jnp.float32).reshape(replica_rows, TOP, D), axis=1)).astype(jnp.bfloat16)
        grad_rows = lax.optimization_barrier(jnp.sum(slot_grad.reshape(total, D)[slots].astype(jnp.float32).reshape(replica_rows, TOP, D), axis=1)).astype(jnp.bfloat16)
        gate_rows = slot_gate.reshape(total)[slots].reshape(replica_rows, TOP)
        new_carry = (carry[0] + part_in.astype(jnp.float32), carry[1] + part_out.astype(jnp.float32))
        return (new_carry, (layer_rows, grad_rows, gate_rows))
    start = (jnp.zeros((EXPERTS, D, 2 * FF), jnp.float32), jnp.zeros((EXPERTS, FF, D), jnp.float32))
    sums, outputs = lax.scan(replica, start, (slot_index, replica_tokens, replica_cots, replica_gates))
    grad_in, grad_out = sums
    layer_out = outputs[0].reshape(TOKENS, D)
    tokens_grad = outputs[1].reshape(TOKENS, D)
    gate_grad = outputs[2].reshape(TOKENS, TOP)
    w_in_new, mom_in_new = lion_update(w_in, mom_in, grad_in)
    w_out_new, mom_out_new = lion_update(w_out, mom_out, grad_out)
    return (layer_out, tokens_grad, gate_grad, w_in_new, w_out_new, mom_in_new, mom_out_new)
```

```python
import jax
import jax.numpy as jnp
from jax import lax
from jax.sharding import PartitionSpec as P

beta_one = 0.9
beta_two = 0.99
learn_rate = 0.02
decay_rate = 0.1

NZ, NY, NC = 2, 4, 2
F32 = jnp.float32
BF16 = jnp.bfloat16


def hop(value, dz=0, dy=0, dc=0):
    pairs = []
    for i in range(NZ * NY * NC):
        z, y, c = i // (NY * NC), (i // NC) % NY, i % NC
        to = ((z + dz) % NZ) * NY * NC + ((y + dy) % NY) * NC + (c + dc) % NC
        pairs.append((i, to))
    return lax.ppermute(value, "expert", pairs)


def lion_update(weight, moment, grad):
    blend = beta_one * moment + (1.0 - beta_one) * grad
    direction = blend / jnp.sqrt(blend * blend + 1.0)
    wide = weight.astype(F32)
    new_weight = (wide - learn_rate * (direction + decay_rate * wide)).astype(BF16)
    new_moment = beta_two * moment + (1.0 - beta_two) * grad
    return (new_weight, new_moment)


def dot(a, b, dims):
    return lax.dot_general(a, b, (dims, ((), ())), preferred_element_type=F32)


def gather_blocks(own):
    near = jnp.concatenate([own, hop(own, dz=1)], axis=0)
    return jnp.concatenate([near, hop(near, dc=1)], axis=0)


def scatter_blocks(part):
    half = part.shape[0] // 2
    near = part[:half] + hop(part[half:].astype(BF16), dc=1).astype(F32)
    rows = half // 2
    return near[:rows] + hop(near[rows:].astype(BF16), dz=1).astype(F32)


def body(tokens, cotangent, expert_ids, gate_probs, w_in, w_out, mom_in, mom_out):
    tok_rows, top_count = expert_ids.shape
    experts = NZ * NY * NC
    cap = 3 * tok_rows * top_count // (2 * experts)
    blocks = NZ * NC
    width = blocks * tok_rows
    ff = w_in.shape[2] // 2
    me = lax.axis_index("expert")
    z, y, c = me // (NY * NC), (me // NC) % NY, me % NC

    full_in = lax.all_gather(w_in, "dp", axis=1, tiled=True)[0]
    full_out = lax.all_gather(w_out, "dp", axis=1, tiled=True)[0]

    meta = jnp.concatenate([expert_ids.T.astype(BF16), gate_probs.T], axis=0)
    meta = gather_blocks(meta[None])
    x_all = gather_blocks(tokens)
    cot_all = gather_blocks(cotangent)
    ids = meta[:, :top_count].astype(jnp.int32)
    gates = meta[:, top_count:].astype(F32)
    steps = jnp.arange(NY, dtype=jnp.int32)
    wanted = z * (NY * NC) + ((y + steps) % NY) * NC + c
    hits = ids[None] == wanted[:, None, None, None]
    member = jnp.any(hits, axis=2)
    gate_of = jnp.sum(jnp.where(hits, gates[None], 0.0), axis=2)
    before = (jnp.arange(tok_rows)[:, None] < jnp.arange(tok_rows)[None, :]).astype(BF16)
    position = dot(
        member.reshape(NY * blocks, tok_rows).astype(BF16), before, ((1,), (0,))
    ).astype(jnp.int32)
    position = jnp.where(member.reshape(NY * blocks, tok_rows), position, -1)
    position = position.reshape(NY, blocks, tok_rows)
    same = jnp.eye(blocks, dtype=bool)
    spread = jnp.where(same[None, :, :, None], position[:, None], -1)
    spread = spread.reshape(NY * blocks, width)
    place = spread[:, None, :] == jnp.arange(cap, dtype=jnp.int32)[None, :, None]
    slots = NY * blocks * cap
    gate_wide = jnp.broadcast_to(
        gate_of.reshape(NY, 1, 1, width), (NY, blocks, cap, width)
    ).reshape(slots, width)
    place = place.reshape(slots, width)
    pick = place.astype(BF16)
    pick_gate = jnp.where(place, gate_wide, 0.0).astype(BF16)

    chunk = blocks * cap

    def to_experts(rows):
        parts = [rows[:chunk]]
        for step in range(1, NY):
            parts.append(hop(rows[step * chunk : (step + 1) * chunk], dy=step))
        return jnp.concatenate(parts, axis=0)

    def from_experts(rows):
        parts = [rows[:chunk]]
        for step in range(1, NY):
            parts.append(hop(rows[step * chunk : (step + 1) * chunk], dy=-step))
        return jnp.concatenate(parts, axis=0)

    expert_in = to_experts(dot(pick, x_all, ((1,), (0,))).astype(BF16))
    out_grad = to_experts(dot(pick_gate, cot_all, ((1,), (0,))).astype(BF16))

    pre = dot(expert_in, full_in, ((1,), (0,)))
    gate_part, up_part = pre[:, :ff], pre[:, ff:]
    sig_part = jax.nn.sigmoid(gate_part)
    activated = gate_part * sig_part
    hidden = (activated * up_part).astype(BF16)
    expert_out = dot(hidden, full_out, ((1,), (0,))).astype(BF16)
    hidden_grad = dot(out_grad, full_out, ((1,), (1,)))
    slope = sig_part * (1.0 + gate_part * (1.0 - sig_part))
    pre_grad = jnp.concatenate(
        [hidden_grad * up_part * slope, hidden_grad * activated], axis=-1
    ).astype(BF16)
    slot_grad = dot(pre_grad, full_in, ((1,), (1,))).astype(BF16)
    term_in = dot(expert_in, pre_grad, ((0,), (0,))).astype(BF16)
    term_out = dot(hidden, out_grad, ((0,), (0,))).astype(BF16)

    layer_rows = from_experts(expert_out)
    grad_rows = from_experts(slot_grad)
    layer_out = scatter_blocks(dot(pick_gate, layer_rows, ((0,), (0,)))).astype(BF16)
    tokens_grad = scatter_blocks(dot(pick, grad_rows, ((0,), (0,)))).astype(BF16)
    inner = dot(layer_rows, cot_all, ((1,), (1,)))
    inner = jnp.sum(
        jnp.where(place, inner, 0.0).reshape(NY, chunk, width), axis=1
    ).reshape(NY, blocks, 1, tok_rows)
    gate_part_grad = jnp.sum(jnp.where(hits, inner, 0.0), axis=0)
    gate_part_grad = gate_part_grad.reshape(blocks * top_count, tok_rows)
    gate_grad = scatter_blocks(gate_part_grad).T.astype(BF16)

    grad_in = lax.psum_scatter(term_in[None], "dp", scatter_dimension=1, tiled=True).astype(F32)
    grad_out = lax.psum_scatter(term_out[None], "dp", scatter_dimension=1, tiled=True).astype(F32)
    w_in_new, mom_in_new = lion_update(w_in, mom_in, grad_in)
    w_out_new, mom_out_new = lion_update(w_out, mom_out, grad_out)
    return (layer_out, tokens_grad, gate_grad, w_in_new, w_out_new, mom_in_new, mom_out_new)


def solution(mesh):
    token = P(("dp", "expert"), None)
    weight = P("expert", "dp", None)
    in_specs = (token, token, token, token, weight, weight, weight, weight)
    out_specs = (token, token, token, weight, weight, weight, weight)
    return jax.shard_map(body, mesh=mesh, in_specs=in_specs, out_specs=out_specs, check_vma=False)
```

```python
import jax
import jax.numpy as jnp
from jax import lax
from jax.sharding import PartitionSpec as P

beta_one = 0.9
beta_two = 0.99
learn_rate = 0.02
decay_rate = 0.1

NZ, NY, NC = 2, 4, 2
NL, NX = 2, 4
F32 = jnp.float32
BF16 = jnp.bfloat16


def hop(value, dz=0, dy=0, dc=0):
    pairs = []
    for i in range(NZ * NY * NC):
        z, y, c = i // (NY * NC), (i // NC) % NY, i % NC
        to = ((z + dz) % NZ) * NY * NC + ((y + dy) % NY) * NC + (c + dc) % NC
        pairs.append((i, to))
    return lax.ppermute(value, "expert", pairs)


def ring(value, dx=0, dz=0):
    pairs = []
    for i in range(NL * NX):
        z, x = i // NX, i % NX
        pairs.append((i, ((z + dz) % NL) * NX + (x + dx) % NX))
    return lax.ppermute(value, "dp", pairs)


def add(*parts):
    total = parts[0].astype(F32)
    for part in parts[1:]:
        total = total + part.astype(F32)
    return total


def gather_rows(own):
    half = own.shape[0] // 2
    far = ring(own, dz=1)
    left, right = ring(own, dx=1), ring(own, dx=-1)
    two = jnp.concatenate([ring(left[:half], dx=1), ring(right[half:], dx=-1)], axis=0)
    far_left, far_right = ring(far, dx=1), ring(far, dx=-1)
    far_two = ring(two, dz=1)
    return jnp.concatenate([own, right, two, left, far, far_right, far_two, far_left], axis=0)


def scatter_rows(terms):
    rows = terms.shape[0] // (NL * NX)
    half = rows // 2
    part = [terms[i * rows : (i + 1) * rows] for i in range(NL * NX)]
    far_a, far_b = ring(part[5], dx=1), ring(part[7], dx=-1)
    two = add(part[2], ring(part[6], dz=1)).astype(BF16)
    in_a, in_b = ring(two[:half], dx=1), ring(two[half:], dx=-1)
    one = jnp.concatenate([add(part[1][:half], in_a).astype(BF16), part[1][half:]], axis=0)
    three = jnp.concatenate([part[3][:half], add(part[3][half:], in_b).astype(BF16)], axis=0)
    far = add(part[4], far_a, far_b).astype(BF16)
    return add(part[0], ring(one, dx=1), ring(three, dx=-1), ring(far, dz=1))


def lion_update(weight, moment, grad):
    blend = beta_one * moment + (1.0 - beta_one) * grad
    direction = blend / jnp.sqrt(blend * blend + 1.0)
    wide = weight.astype(F32)
    new_weight = (wide - learn_rate * (direction + decay_rate * wide)).astype(BF16)
    new_moment = beta_two * moment + (1.0 - beta_two) * grad
    return (new_weight, new_moment)


def dot(a, b, dims):
    return lax.dot_general(a, b, (dims, ((), ())), preferred_element_type=F32)


def gather_blocks(own):
    near = jnp.concatenate([own, hop(own, dz=1)], axis=0)
    return jnp.concatenate([near, hop(near, dc=1)], axis=0)


def scatter_blocks(part):
    half = part.shape[0] // 2
    near = part[:half] + hop(part[half:].astype(BF16), dc=1).astype(F32)
    rows = half // 2
    return near[:rows] + hop(near[rows:].astype(BF16), dz=1).astype(F32)


def body(tokens, cotangent, expert_ids, gate_probs, w_in, w_out, mom_in, mom_out):
    tok_rows, top_count = expert_ids.shape
    experts = NZ * NY * NC
    cap = 3 * tok_rows * top_count // (2 * experts)
    blocks = NZ * NC
    width = blocks * tok_rows
    ff = w_in.shape[2] // 2
    ff_rows = w_out.shape[1]
    me = lax.axis_index("expert")
    z, y, c = me // (NY * NC), (me // NC) % NY, me % NC

    dp = lax.axis_index("dp")
    zl, x = dp // NX, dp % NX
    groups = [[k * NX + i for i in range(NX)] for k in range(NL)]

    full_in = gather_rows(w_in[0])
    out_far = ring(w_out[0], dz=1)
    pair = jnp.where(
        zl == 0, jnp.stack([w_out[0], out_far]), jnp.stack([out_far, w_out[0]])
    )
    full_out = lax.all_gather(pair, "dp", axis=1, tiled=True, axis_index_groups=groups)
    full_out = full_out.reshape(ff_rows * NL * NX, -1)
    wide = tokens.shape[1] // (NL * NX)

    def block_of(step):
        return ((zl + step // NX) % NL) * NX + (x + step % NX) % NX

    turned = jnp.concatenate(
        [lax.dynamic_slice_in_dim(tokens, block_of(i) * wide, wide, 1) for i in range(NL * NX)],
        axis=1,
    )

    meta = jnp.concatenate([expert_ids.T.astype(BF16), gate_probs.T], axis=0)
    meta = gather_blocks(meta[None])
    x_all = gather_blocks(turned)
    cot_all = gather_blocks(cotangent)
    ids = meta[:, :top_count].astype(jnp.int32)
    gates = meta[:, top_count:].astype(F32)
    steps = jnp.arange(NY, dtype=jnp.int32)
    wanted = z * (NY * NC) + ((y + steps) % NY) * NC + c
    hits = ids[None] == wanted[:, None, None, None]
    member = jnp.any(hits, axis=2)
    gate_of = jnp.sum(jnp.where(hits, gates[None], 0.0), axis=2)
    before = (jnp.arange(tok_rows)[:, None] < jnp.arange(tok_rows)[None, :]).astype(BF16)
    position = dot(
        member.reshape(NY * blocks, tok_rows).astype(BF16), before, ((1,), (0,))
    ).astype(jnp.int32)
    position = jnp.where(member.reshape(NY * blocks, tok_rows), position, -1)
    position = position.reshape(NY, blocks, tok_rows)
    same = jnp.eye(blocks, dtype=bool)
    spread = jnp.where(same[None, :, :, None], position[:, None], -1)
    spread = spread.reshape(NY * blocks, width)
    place = spread[:, None, :] == jnp.arange(cap, dtype=jnp.int32)[None, :, None]
    slots = NY * blocks * cap
    gate_wide = jnp.broadcast_to(
        gate_of.reshape(NY, 1, 1, width), (NY, blocks, cap, width)
    ).reshape(slots, width)
    place = place.reshape(slots, width)
    pick = place.astype(BF16)
    pick_gate = jnp.where(place, gate_wide, 0.0).astype(BF16)

    chunk = blocks * cap

    def to_experts(rows):
        parts = [rows[:chunk]]
        for step in range(1, NY):
            parts.append(hop(rows[step * chunk : (step + 1) * chunk], dy=step))
        return jnp.concatenate(parts, axis=0)

    def from_experts(rows):
        parts = [rows[:chunk]]
        for step in range(1, NY):
            parts.append(hop(rows[step * chunk : (step + 1) * chunk], dy=-step))
        return jnp.concatenate(parts, axis=0)

    expert_in = to_experts(dot(pick, x_all, ((1,), (0,))).astype(BF16))
    out_grad = to_experts(dot(pick_gate, cot_all, ((1,), (0,))).astype(BF16))

    pre = dot(expert_in, full_in, ((1,), (0,)))
    gate_part, up_part = pre[:, :ff], pre[:, ff:]
    sig_part = jax.nn.sigmoid(gate_part)
    activated = gate_part * sig_part
    hidden = (activated * up_part).astype(BF16)
    expert_out = dot(hidden, full_out, ((1,), (0,))).astype(BF16)
    hidden_grad = dot(out_grad, full_out, ((1,), (1,)))
    slope = sig_part * (1.0 + gate_part * (1.0 - sig_part))
    pre_grad = jnp.concatenate(
        [hidden_grad * up_part * slope, hidden_grad * activated], axis=-1
    ).astype(BF16)
    slot_grad = dot(pre_grad, full_in, ((1,), (1,))).astype(BF16)
    term_in = dot(expert_in, pre_grad, ((0,), (0,))).astype(BF16)
    term_out = dot(hidden, out_grad, ((0,), (0,))).astype(BF16)

    layer_rows = from_experts(expert_out)
    grad_rows = from_experts(slot_grad)
    layer_out = scatter_blocks(dot(pick_gate, layer_rows, ((0,), (0,)))).astype(BF16)
    turned_grad = scatter_blocks(dot(pick, grad_rows, ((0,), (0,)))).astype(BF16)

    def step_of(block):
        return ((block // NX - zl) % NL) * NX + (block % NX - x) % NX

    tokens_grad = jnp.concatenate(
        [
            lax.dynamic_slice_in_dim(turned_grad, step_of(i) * wide, wide, 1)
            for i in range(NL * NX)
        ],
        axis=1,
    )
    inner = dot(layer_rows, cot_all, ((1,), (1,)))
    inner = jnp.sum(
        jnp.where(place, inner, 0.0).reshape(NY, chunk, width), axis=1
    ).reshape(NY, blocks, 1, tok_rows)
    gate_part_grad = jnp.sum(jnp.where(hits, inner, 0.0), axis=0)
    gate_part_grad = gate_part_grad.reshape(blocks * top_count, tok_rows)
    gate_grad = scatter_blocks(gate_part_grad).T.astype(BF16)

    grad_in = scatter_rows(term_in)[None]
    halves = lax.psum_scatter(
        term_out.reshape(NL, ff_rows * NX, -1),
        "dp",
        scatter_dimension=1,
        tiled=True,
        axis_index_groups=groups,
    )
    kept = lax.dynamic_index_in_dim(halves, zl, 0, True)
    given = lax.dynamic_index_in_dim(halves, 1 - zl, 0, True)
    grad_out = add(kept, ring(given, dz=1))
    w_in_new, mom_in_new = lion_update(w_in, mom_in, grad_in)
    w_out_new, mom_out_new = lion_update(w_out, mom_out, grad_out)
    return (layer_out, tokens_grad, gate_grad, w_in_new, w_out_new, mom_in_new, mom_out_new)


def solution(mesh):
    token = P(("dp", "expert"), None)
    weight = P("expert", "dp", None)
    in_specs = (token, token, token, token, weight, weight, weight, weight)
    out_specs = (token, token, token, weight, weight, weight, weight)
    return jax.shard_map(body, mesh=mesh, in_specs=in_specs, out_specs=out_specs, check_vma=False)
```

```python
import functools

import jax
import jax.numpy as jnp
from jax import lax
from jax.experimental import pallas as pl
from jax.experimental.pallas import tpu as pltpu
from jax.sharding import PartitionSpec as P

beta_one = 0.9
beta_two = 0.99
learn_rate = 0.02
decay_rate = 0.1

NZ, NY, NC = 2, 4, 2
NL, NX = 2, 4
F32 = jnp.float32
BF16 = jnp.bfloat16


def hop(value, dz=0, dy=0, dc=0):
    pairs = []
    for i in range(NZ * NY * NC):
        z, y, c = i // (NY * NC), (i // NC) % NY, i % NC
        to = ((z + dz) % NZ) * NY * NC + ((y + dy) % NY) * NC + (c + dc) % NC
        pairs.append((i, to))
    return lax.ppermute(value, "expert", pairs)


def over_y(value):
    groups = [
        [(z * NY + y) * NC + c for y in range(NY)] for z in range(NZ) for c in range(NC)
    ]
    return lax.all_to_all(value, "expert", 0, 0, tiled=True, axis_index_groups=groups)


def ring(value, dx=0, dz=0):
    pairs = []
    for i in range(NL * NX):
        z, x = i // NX, i % NX
        pairs.append((i, ((z + dz) % NL) * NX + (x + dx) % NX))
    return lax.ppermute(value, "dp", pairs)


def after(value, *earlier):
    return lax.optimization_barrier((value, *earlier))[0]


def add(*parts):
    total = parts[0].astype(F32)
    for part in parts[1:]:
        total = total + part.astype(F32)
    return total


def lion_update(weight, moment, grad):
    blend = beta_one * moment + (1.0 - beta_one) * grad
    direction = blend / jnp.sqrt(blend * blend + 1.0)
    wide = weight.astype(F32)
    new_weight = (wide - learn_rate * (direction + decay_rate * wide)).astype(BF16)
    new_moment = beta_two * moment + (1.0 - beta_two) * grad
    return (new_weight, new_moment)


def dot(a, b, dims):
    return lax.dot_general(a, b, (dims, ((), ())), preferred_element_type=F32)


def call(kernel, outs, ins, hbm_ins=0, hbm_outs=0, scratch=()):
    vmem, stay = pl.BlockSpec(memory_space=pltpu.VMEM), pl.BlockSpec(memory_space=pl.ANY)
    specs = [pl.BlockSpec(memory_space=pltpu.SMEM)]
    specs += [vmem] * (len(ins) - 1 - hbm_ins) + [stay] * hbm_ins
    return pl.pallas_call(
        kernel,
        out_shape=[jax.ShapeDtypeStruct(*out) for out in outs],
        in_specs=specs,
        out_specs=[vmem] * (len(outs) - hbm_outs) + [stay] * hbm_outs,
        scratch_shapes=list(scratch),
        compiler_params=pltpu.CompilerParams(vmem_limit_bytes=56 << 20),
    )(*ins)


def place_copies(order, pieces, target, rows, sems, base):
    copies = []
    for i, (ref, first, count, step, within) in enumerate(pieces):
        at = pl.multiple_of(order[step] * rows, rows) + within
        copies.append(
            pltpu.make_async_copy(
                ref.at[pl.ds(first, count)], target.at[pl.ds(at, count)], sems.at[base + i]
            )
        )
    return copies


def pre_kernel(count, order, *refs):
    parts, shards = refs[:count], refs[count : count + 9]
    pre, full, rows_out, rows, weight, sems, out_sems = refs[count + 9 :]
    size = parts[0].shape[0] // NY
    shard = shards[0].shape[0]
    half = shard // 2
    row_copies = [
        pltpu.make_async_copy(
            part.at[pl.ds(i * size, size)],
            rows.at[pl.ds((i * count + j) * size, size)],
            sems.at[i * count + j],
        )
        for i in range(NY)
        for j, part in enumerate(parts)
    ]
    own, right, two_a, two_b, left, far, far_right, far_two, far_left = shards
    near = [
        (own, 0, shard, 0, 0), (right, 0, shard, 1, 0), (two_a, 0, half, 2, 0),
        (two_b, 0, half, 2, half), (left, 0, shard, 3, 0),
    ]
    away = [
        (far, 0, shard, 4, 0), (far_right, 0, shard, 5, 0), (far_two, 0, shard, 6, 0),
        (far_left, 0, shard, 7, 0),
    ]
    near = place_copies(order, near, weight, shard, sems, NY * count)
    away = place_copies(order, away, weight, shard, sems, NY * count + 5)
    for copy in row_copies + near + away:
        copy.start()
    plane = shard * NX
    width = weight.shape[1] // 3

    def product(which, tile):
        at = pl.multiple_of(which * plane, plane)
        columns = slice(tile * width, (tile + 1) * width)
        return dot(rows[:, pl.ds(at, plane)], weight[pl.ds(at, plane), columns], ((1,), (0,)))

    for copy in row_copies + near:
        copy.wait()
    out_rows = pltpu.make_async_copy(rows, rows_out, out_sems.at[0])
    out_rows.start()
    here = order[0] // NX
    for tile in range(3):
        pre[:, tile * width : (tile + 1) * width] = product(here, tile)
    for copy in away:
        copy.wait()
    out_full = pltpu.make_async_copy(weight, full, out_sems.at[1])
    out_full.start()
    for tile in range(3):
        pre[:, tile * width : (tile + 1) * width] += product(1 - here, tile)
    out_rows.wait()
    out_full.wait()


def out_kernel(order, pre, own, far, left, right, two_a, two_b, *refs):
    out, hidden, full, weight, sems, out_sem = refs
    shard = own.shape[0]
    pieces = [
        (own, 0, shard, 0, 0), (right, 0, shard, 1, 0), (two_a, 0, shard, 2, 0),
        (left, 0, shard, 3, 0), (far, 0, shard, 4, 0), (right, shard, shard, 5, 0),
        (two_b, 0, shard, 6, 0), (left, shard, shard, 7, 0),
    ]
    copies = place_copies(order, pieces, weight, shard, sems, 0)
    for copy in copies:
        copy.start()
    ff = hidden.shape[1]
    gate = pre[:, :ff]
    hidden[...] = (gate * jax.nn.sigmoid(gate) * pre[:, ff:]).astype(BF16)
    for copy in copies:
        copy.wait()
    out_full = pltpu.make_async_copy(weight, full, out_sem)
    out_full.start()
    width = weight.shape[1] // 4
    for tile in range(4):
        columns = slice(tile * width, (tile + 1) * width)
        out[:, columns] = dot(hidden[...], weight[:, columns], ((1,), (0,))).astype(BF16)
    out_full.wait()


def routing(wanted, metas):
    top = metas[0].shape[0] // 2
    rows = metas[0].shape[1]
    ids = [meta[...].astype(F32)[:top] for meta in metas]
    gates = [meta[...].astype(F32)[top:] for meta in metas]
    hits = [[block == wanted[step].astype(F32) for step in range(NY)] for block in ids]
    member, weight = [], []
    for block, gate in zip(hits, gates, strict=True):
        for hit in block:
            member.append(jnp.max(jnp.where(hit, 1.0, 0.0), axis=0, keepdims=True))
            weight.append(jnp.sum(jnp.where(hit, gate, 0.0), axis=0, keepdims=True))
    below = lax.broadcasted_iota(jnp.int32, (rows, rows), 0)
    right = lax.broadcasted_iota(jnp.int32, (rows, rows), 1)
    before = jnp.where(below < right, 1.0, 0.0).astype(BF16)
    found = jnp.concatenate(member, axis=0)
    position = dot(found.astype(BF16), before, ((1,), (0,)))
    position = jnp.where(found > 0.5, position, -1.0).astype(jnp.int32)
    return hits, weight, position


def one_hot(position, weight, block, cap):
    rows = position.shape[1]
    slot = lax.broadcasted_iota(jnp.int32, (cap, rows), 0)
    parts = []
    for step in range(NY):
        at = block * NY + step
        value = 1.0 if weight is None else weight[at]
        parts.append(jnp.where(slot == position[at : at + 1], value, 0.0))
    return jnp.concatenate(parts, axis=0)


def gather_kernel(weighted, cap, wanted, *refs):
    count = len(refs) // 2
    metas, rows, out = refs[:count], refs[count : 2 * count], refs[2 * count]
    _, weight, position = routing(wanted, metas)
    for block in range(count):
        pick = one_hot(position, weight if weighted else None, block, cap).astype(BF16)
        got = dot(pick, rows[block][...], ((1,), (0,))).astype(BF16)
        for step in range(NY):
            at = (step * count + block) * cap
            out[at : at + cap] = got[step * cap : (step + 1) * cap]


def combine_kernel(weighted, cap, count, wanted, *refs):
    metas, slots, refs = refs[:count], refs[count], refs[count + 1 :]
    hits, weight, position = routing(wanted, metas)
    grads = []
    cots, outs = (refs[:count], refs[count:]) if weighted else ((), refs)
    other = outs[count // 2]
    for block in range(count):
        pick = one_hot(position, weight if weighted else None, block, cap).astype(BF16)
        rows = jnp.concatenate(
            [slots[pl.ds((step * count + block) * cap, cap)] for step in range(NY)],
            axis=0,
        )
        total = dot(pick, rows, ((0,), (0,)))
        side = block // 2
        if block % 2 == 0:
            outs[side][...] = total
        else:
            size = total.shape[0]
            other[side * size : (side + 1) * size] = total.astype(BF16)
        if weighted:
            inner = dot(rows, cots[block][...], ((1,), (1,)))
            inner = jnp.where(one_hot(position, None, block, cap) > 0.5, inner, 0.0)
            grad = 0.0
            for step in range(NY):
                value = jnp.sum(inner[step * cap : (step + 1) * cap], axis=0, keepdims=True)
                grad = grad + jnp.where(hits[block][step], value, 0.0)
            grads.append(grad)
    if weighted:
        outs[3][...] = jnp.concatenate(grads[::2], axis=0)
        outs[4][...] = jnp.concatenate(grads[1::2], axis=0)


def body(tokens, cotangent, expert_ids, gate_probs, w_in, w_out, mom_in, mom_out):
    tok_rows, top_count = expert_ids.shape
    experts = NZ * NY * NC
    cap = 3 * tok_rows * top_count // (2 * experts)
    blocks = NZ * NC
    ff = w_in.shape[2] // 2
    chunk = blocks * cap
    me = lax.axis_index("expert")
    z, y, c = me // (NY * NC), (me // NC) % NY, me % NC
    dp = lax.axis_index("dp")
    zl, x = dp // NX, dp % NX

    def index_of(step):
        return ((zl + step // NX) % NL) * NX + (x + step % NX) % NX

    def take_rows(full, step):
        rows = full.shape[0] // (NL * NX)
        return lax.dynamic_slice_in_dim(full, index_of(step) * rows, rows, 0)

    steps = jnp.arange(NL * NX, dtype=jnp.int32)
    order = index_of(steps)
    steps = jnp.arange(NY, dtype=jnp.int32)
    wanted = z * (NY * NC) + steps * NC + c
    model = tokens.shape[1]

    meta = jnp.concatenate([expert_ids.T.astype(BF16), gate_probs.T], axis=0)
    own_in, own_out = w_in[0], w_out[0]
    meta_z = hop(meta, dz=1)
    meta_c, tok_c = hop(meta, dc=1), hop(tokens, dc=1)
    tok_z = hop(tokens, dz=1)
    meta_zc = hop(meta_z, dc=1)
    metas = [meta, meta_c, meta_z, meta_zc]

    def gather(weighted, metas, rows):
        outs = [((len(rows) * cap * NY, model), BF16)]
        return call(
            functools.partial(gather_kernel, weighted, cap), outs, [wanted, *metas, *rows]
        )[0]

    near_part = over_y(gather(False, metas[:2], [tokens, tok_c]))
    in_left, in_right = ring(own_in, dx=1), ring(own_in, dx=-1)
    tok_zc = hop(after(tok_z, in_left, in_right), dc=1)
    away_rows = gather(False, metas[2:], [tok_z, tok_zc])
    away_part = over_y(away_rows)

    half = own_in.shape[0] // 2
    in_far = ring(after(own_in, tok_z, meta_z), dz=1)
    two_a, two_b = ring(in_left[:half], dx=1), ring(in_right[half:], dx=-1)
    near_far = after(in_far, two_a, two_b)
    in_far_left, in_far_right = ring(near_far, dx=1), ring(near_far, dx=-1)
    cot_in = after(cotangent, in_far)
    cot_z = hop(cot_in, dz=1)
    cot_c = hop(after(cotangent, away_rows), dc=1)
    cot_zc = hop(cot_z, dc=1)
    cots = [cotangent, cot_c, cot_z, cot_zc]
    out_far = ring(after(own_out, cot_z), dz=1)
    in_far_two = ring(after(jnp.concatenate([two_a, two_b], axis=0), out_far), dz=1)
    cot_z_late, cot_zc_late = lax.optimization_barrier(
        (cot_z, cot_zc, in_far_left, in_far_right)
    )[:2]
    cot_rows = gather(True, metas, [cotangent, cot_c, cot_z_late, cot_zc_late])
    out_grad = over_y(cot_rows)
    out_pair = jnp.concatenate([own_out, out_far], axis=0)
    out_pair = after(out_pair, in_far_left, in_far_right)
    out_left, out_right = ring(out_pair, dx=1), ring(out_pair, dx=-1)
    oh = own_out.shape[0]

    parts = [near_part, away_part]
    shards = [
        own_in, in_right, two_a, two_b, in_left, in_far, in_far_right, in_far_two, in_far_left,
    ]
    shards = list(lax.optimization_barrier((*shards, cot_rows))[:9])
    slots = NY * chunk
    pre, full_in, expert_in = call(
        functools.partial(pre_kernel, len(parts)),
        [((slots, 2 * ff), F32), ((model, 2 * ff), BF16), ((slots, model), BF16)],
        [order, *parts, *shards],
        hbm_ins=len(parts) + 9,
        hbm_outs=2,
        scratch=[
            pltpu.VMEM((slots, model), BF16),
            pltpu.VMEM((model, 2 * ff), BF16),
            pltpu.SemaphoreType.DMA((NY * len(parts) + 9,)),
            pltpu.SemaphoreType.DMA((2,)),
        ],
    )
    out_left, out_right = lax.optimization_barrier((out_left, out_right, pre))[:2]
    out_two_a, out_two_b = ring(out_left[:oh], dx=1), ring(out_right[oh:], dx=-1)
    expert_out, hidden, full_out = call(
        out_kernel,
        [((slots, model), BF16), ((slots, ff), BF16), ((ff, model), BF16)],
        [order, pre, own_out, out_far, out_left, out_right, out_two_a, out_two_b],
        hbm_ins=6,
        hbm_outs=1,
        scratch=[
            pltpu.VMEM((ff, model), BF16),
            pltpu.SemaphoreType.DMA((8,)),
            pltpu.SemaphoreType.DMA,
        ],
    )
    layer_rows = over_y(expert_out)
    term_out = dot(hidden, out_grad, ((0,), (0,))).astype(BF16)
    gate_part, up_part = pre[:, :ff], pre[:, ff:]
    sig_part = jax.nn.sigmoid(gate_part)
    activated = gate_part * sig_part

    def combine(weighted, rows, metas, cots):
        count = len(metas)
        outs = [((tok_rows, model), F32)] * (count // 2)
        outs += [((count // 2 * tok_rows, model), BF16)]
        outs += [((2 * top_count, tok_rows), F32)] * (2 if weighted else 0)
        return call(
            functools.partial(combine_kernel, weighted, cap, count),
            outs,
            [wanted, *metas, rows, *cots],
        )

    def out_pair_of(step):
        return [take_rows(term_out, step), take_rows(term_out, NX + step)]

    two_a, two_b = out_pair_of(2)
    got_a, got_b = ring(two_a, dx=1), ring(two_b, dx=-1)
    one, one_far = out_pair_of(1)
    three, three_far = out_pair_of(3)
    to_right = jnp.concatenate([add(one, got_a).astype(BF16), one_far], axis=0)
    to_left = jnp.concatenate([three, add(three_far, got_b).astype(BF16)], axis=0)

    hidden_grad = dot(after(out_grad, term_out), full_out, ((1,), (1,)))
    slope = sig_part * (1.0 + gate_part * (1.0 - sig_part))
    pre_grad = jnp.concatenate(
        [hidden_grad * up_part * slope, hidden_grad * activated], axis=-1
    ).astype(BF16)
    term_in = dot(after(expert_in, got_a, got_b), pre_grad, ((0,), (0,))).astype(BF16)
    slot_grad = dot(after(pre_grad, term_in), full_in, ((1,), (1,))).astype(BF16)
    slot_grad = slot_grad.reshape(NY, 2, chunk // 2, model)
    part = [take_rows(term_in, step) for step in range(NL * NX)]
    part_a, part_b = after(part[5], got_a, got_b), after(part[7], got_a, got_b)
    far_a, far_b = ring(part_a, dx=1), ring(part_b, dx=-1)
    away_grad = over_y(after(slot_grad[:, 1].reshape(-1, model), layer_rows))
    near_grad = over_y(after(slot_grad[:, 0].reshape(-1, model), away_grad, far_a, far_b))
    two = add(part[2], ring(part[6], dz=1)).astype(BF16)
    two = after(two, far_a, far_b)
    in_a, in_b = ring(two[:half], dx=1), ring(two[half:], dx=-1)
    far = add(part[4], far_a, far_b).astype(BF16)
    far_back = ring(far, dz=1)
    from_left, from_right = ring(after(to_right, far_a), dx=1), ring(after(to_left, far_b), dx=-1)
    one = jnp.concatenate([add(part[1][:half], in_a).astype(BF16), part[1][half:]], axis=0)
    three = jnp.concatenate([part[3][:half], add(part[3][half:], in_b).astype(BF16)], axis=0)
    one, three = after(one, from_left), after(three, from_right)
    one_back, three_back = ring(one, dx=1), ring(three, dx=-1)
    zero, zero_far = out_pair_of(0)
    out_far_sum = add(zero_far, from_left[oh:], from_right[oh:]).astype(BF16)
    out_back = ring(after(out_far_sum, far_back), dz=1)
    grad_out = add(zero, from_left[:oh], from_right[:oh], out_back)[None]
    grad_in = add(part[0], one_back, three_back, far_back)[None]

    mine, mine_z, other, gate_mine, gate_other = combine(True, layer_rows, metas, cots)
    got = hop(other, dc=1)
    back = hop((mine_z + got[tok_rows:].astype(F32)).astype(BF16), dz=1)
    layer_back = back
    layer_out = add(mine, got[:tok_rows], back).astype(BF16)
    gate_near = gate_mine + hop(gate_other, dc=1)

    mine_z, other = combine(False, after(away_grad, back), metas[2:], ())
    away_sum = (mine_z + hop(other, dc=1).astype(F32)).astype(BF16)
    back = hop(away_sum, dz=1)
    mine, other = combine(False, near_grad, metas[:2], ())
    tokens_grad = add(mine, hop(other, dc=1), back).astype(BF16)
    gate_far = hop(after(gate_near[top_count:], layer_back), dz=1)
    gate_grad = (gate_near[:top_count] + gate_far).T.astype(BF16)

    w_in_new, mom_in_new = lion_update(w_in, mom_in, grad_in)
    w_out_new, mom_out_new = lion_update(w_out, mom_out, grad_out)
    return (layer_out, tokens_grad, gate_grad, w_in_new, w_out_new, mom_in_new, mom_out_new)


def solution(mesh):
    token = P(("dp", "expert"), None)
    weight = P("expert", "dp", None)
    in_specs = (token, token, token, token, weight, weight, weight, weight)
    out_specs = (token, token, token, weight, weight, weight, weight)
    return jax.shard_map(body, mesh=mesh, in_specs=in_specs, out_specs=out_specs, check_vma=False)
```

```python
import functools

import jax
import jax.numpy as jnp
from jax import lax
from jax.experimental import pallas as pl
from jax.experimental.pallas import tpu as pltpu
from jax.sharding import PartitionSpec as P

beta_one = 0.9
beta_two = 0.99
learn_rate = 0.02
decay_rate = 0.1

NZ, NY, NC = 2, 4, 2
NL, NX = 2, 4
TOP = 4
PAD = 16
F32 = jnp.float32
BF16 = jnp.bfloat16


def hop(value, dz=0, dy=0, dc=0):
    pairs = []
    for i in range(NZ * NY * NC):
        z, y, c = i // (NY * NC), (i // NC) % NY, i % NC
        to = ((z + dz) % NZ) * NY * NC + ((y + dy) % NY) * NC + (c + dc) % NC
        pairs.append((i, to))
    return lax.ppermute(value, "expert", pairs)


def over_y(value):
    groups = [
        [(z * NY + y) * NC + c for y in range(NY)] for z in range(NZ) for c in range(NC)
    ]
    return lax.all_to_all(value, "expert", 0, 0, tiled=True, axis_index_groups=groups)


def ring(value, dx=0, dz=0):
    pairs = []
    for i in range(NL * NX):
        z, x = i // NX, i % NX
        pairs.append((i, ((z + dz) % NL) * NX + (x + dx) % NX))
    return lax.ppermute(value, "dp", pairs)


def after(value, *earlier):
    return lax.optimization_barrier((value, *earlier))[0]


def add(*parts):
    total = parts[0].astype(F32)
    for part in parts[1:]:
        total = total + part.astype(F32)
    return total


def lion_update(weight, moment, grad):
    blend = beta_one * moment + (1.0 - beta_one) * grad
    direction = blend / jnp.sqrt(blend * blend + 1.0)
    wide = weight.astype(F32)
    new_weight = (wide - learn_rate * (direction + decay_rate * wide)).astype(BF16)
    new_moment = beta_two * moment + (1.0 - beta_two) * grad
    return (new_weight, new_moment)


def dot(a, b, dims):
    return lax.dot_general(a, b, (dims, ((), ())), preferred_element_type=F32)


def at_row(row, _):
    return row, 0


def call(kernel, outs, ins, metas=0, hbm_ins=0, hbm_outs=0, scratch=()):
    vmem, stay = pl.BlockSpec(memory_space=pltpu.VMEM), pl.BlockSpec(memory_space=pl.ANY)
    specs = [pl.BlockSpec(memory_space=pltpu.SMEM)]
    for table in ins[1 : 1 + metas]:
        last = table.shape[0] // PAD - 1
        specs.append(pl.BlockSpec((PAD, table.shape[0] - PAD), functools.partial(at_row, last)))
    specs += [vmem] * (len(ins) - 1 - metas - hbm_ins) + [stay] * hbm_ins
    return pl.pallas_call(
        kernel,
        out_shape=[jax.ShapeDtypeStruct(*out) for out in outs],
        grid=(1,) if metas else (),
        in_specs=specs,
        out_specs=[vmem] * (len(outs) - hbm_outs) + [stay] * hbm_outs,
        scratch_shapes=list(scratch),
        compiler_params=pltpu.CompilerParams(vmem_limit_bytes=56 << 20),
    )(*ins)


def place_copies(order, pieces, target, rows, sems, base):
    copies = []
    for i, (ref, first, count, step, within) in enumerate(pieces):
        at = pl.multiple_of(order[step] * rows, rows) + within
        copies.append(
            pltpu.make_async_copy(
                ref.at[pl.ds(first, count)], target.at[pl.ds(at, count)], sems.at[base + i]
            )
        )
    return copies


def pre_kernel(count, order, *refs):
    parts, shards = refs[:count], refs[count : count + 9]
    pre, full, rows_out, rows, weight, sems, out_sems = refs[count + 9 :]
    size = parts[0].shape[0] // NY
    shard = shards[0].shape[0]
    half = shard // 2
    row_copies = [
        pltpu.make_async_copy(
            part.at[pl.ds(i * size, size)],
            rows.at[pl.ds((i * count + j) * size, size)],
            sems.at[i * count + j],
        )
        for i in range(NY)
        for j, part in enumerate(parts)
    ]
    own, right, two_a, two_b, left, far, far_right, far_two, far_left = shards
    near = [
        (own, 0, shard, 0, 0), (right, 0, shard, 1, 0), (two_a, 0, half, 2, 0),
        (two_b, 0, half, 2, half), (left, 0, shard, 3, 0),
    ]
    away = [
        (far, 0, shard, 4, 0), (far_right, 0, shard, 5, 0), (far_two, 0, shard, 6, 0),
        (far_left, 0, shard, 7, 0),
    ]
    near = place_copies(order, near, weight, shard, sems, NY * count)
    away = place_copies(order, away, weight, shard, sems, NY * count + 5)
    for copy in row_copies + near + away:
        copy.start()
    plane = shard * NX
    width = weight.shape[1] // 3

    def product(which, tile):
        at = pl.multiple_of(which * plane, plane)
        columns = slice(tile * width, (tile + 1) * width)
        return dot(rows[:, pl.ds(at, plane)], weight[pl.ds(at, plane), columns], ((1,), (0,)))

    for copy in row_copies + near:
        copy.wait()
    out_rows = pltpu.make_async_copy(rows, rows_out, out_sems.at[0])
    out_rows.start()
    here = order[0] // NX
    for tile in range(3):
        pre[:, tile * width : (tile + 1) * width] = product(here, tile)
    for copy in away:
        copy.wait()
    out_full = pltpu.make_async_copy(weight, full, out_sems.at[1])
    out_full.start()
    for tile in range(3):
        pre[:, tile * width : (tile + 1) * width] += product(1 - here, tile)
    out_rows.wait()
    out_full.wait()


def out_kernel(order, pre, own, far, left, right, two_a, two_b, *refs):
    out, hidden, full, weight, sems, out_sem = refs
    shard = own.shape[0]
    pieces = [
        (own, 0, shard, 0, 0), (right, 0, shard, 1, 0), (two_a, 0, shard, 2, 0),
        (left, 0, shard, 3, 0), (far, 0, shard, 4, 0), (right, shard, shard, 5, 0),
        (two_b, 0, shard, 6, 0), (left, shard, shard, 7, 0),
    ]
    copies = place_copies(order, pieces, weight, shard, sems, 0)
    for copy in copies:
        copy.start()
    ff = hidden.shape[1]
    gate = pre[:, :ff]
    hidden[...] = (gate * jax.nn.sigmoid(gate) * pre[:, ff:]).astype(BF16)
    for copy in copies:
        copy.wait()
    out_full = pltpu.make_async_copy(weight, full, out_sem)
    out_full.start()
    width = weight.shape[1] // 4
    for tile in range(4):
        columns = slice(tile * width, (tile + 1) * width)
        out[:, columns] = dot(hidden[...], weight[:, columns], ((1,), (0,))).astype(BF16)
    out_full.wait()


def routing(wanted, metas):
    top = TOP
    rows = metas[0].shape[1]
    tables = [meta[...].astype(F32) for meta in metas]
    ids = [table[:top] for table in tables]
    gates = [table[top : 2 * top] for table in tables]
    hits = [[block == wanted[step].astype(F32) for step in range(NY)] for block in ids]
    member, weight = [], []
    for block, gate in zip(hits, gates, strict=True):
        for hit in block:
            member.append(jnp.max(jnp.where(hit, 1.0, 0.0), axis=0, keepdims=True))
            weight.append(jnp.sum(jnp.where(hit, gate, 0.0), axis=0, keepdims=True))
    below = lax.broadcasted_iota(jnp.int32, (rows, rows), 0)
    right = lax.broadcasted_iota(jnp.int32, (rows, rows), 1)
    before = jnp.where(below < right, 1.0, 0.0).astype(BF16)
    found = jnp.concatenate(member, axis=0)
    position = dot(found.astype(BF16), before, ((1,), (0,)))
    position = jnp.where(found > 0.5, position, -1.0).astype(jnp.int32)
    return hits, weight, position


def one_hot(position, weight, block, cap):
    rows = position.shape[1]
    slot = lax.broadcasted_iota(jnp.int32, (cap, rows), 0)
    parts = []
    for step in range(NY):
        at = block * NY + step
        value = 1.0 if weight is None else weight[at]
        parts.append(jnp.where(slot == position[at : at + 1], value, 0.0))
    return jnp.concatenate(parts, axis=0)


def gather_kernel(weighted, cap, wanted, *refs):
    count = len(refs) // 2
    metas, rows, out = refs[:count], refs[count : 2 * count], refs[2 * count]
    _, weight, position = routing(wanted, metas)
    for block in range(count):
        pick = one_hot(position, weight if weighted else None, block, cap).astype(BF16)
        got = dot(pick, rows[block][: pick.shape[1]], ((1,), (0,))).astype(BF16)
        for step in range(NY):
            at = (step * count + block) * cap
            out[at : at + cap] = got[step * cap : (step + 1) * cap]


def combine_kernel(weighted, cap, count, wanted, *refs):
    metas, slots, refs = refs[:count], refs[count], refs[count + 1 :]
    hits, weight, position = routing(wanted, metas)
    grads = []
    cots, outs = (refs[:count], refs[count:]) if weighted else ((), refs)
    other = outs[count // 2]
    for block in range(count):
        pick = one_hot(position, weight if weighted else None, block, cap).astype(BF16)
        rows = jnp.concatenate(
            [slots[pl.ds((step * count + block) * cap, cap)] for step in range(NY)],
            axis=0,
        )
        total = dot(pick, rows, ((0,), (0,)))
        side = block // 2
        if block % 2 == 0:
            outs[side][...] = total
        else:
            size = total.shape[0]
            other[side * size : (side + 1) * size] = total.astype(BF16)
        if weighted:
            inner = dot(rows, cots[block][...], ((1,), (1,)))
            inner = jnp.where(one_hot(position, None, block, cap) > 0.5, inner, 0.0)
            grad = 0.0
            for step in range(NY):
                value = jnp.sum(inner[step * cap : (step + 1) * cap], axis=0, keepdims=True)
                grad = grad + jnp.where(hits[block][step], value, 0.0)
            grads.append(grad)
    if weighted:
        outs[3][...] = jnp.concatenate(grads[::2], axis=0)
        outs[4][...] = jnp.concatenate(grads[1::2], axis=0)


def body(tokens, cotangent, expert_ids, gate_probs, w_in, w_out, mom_in, mom_out):
    tok_rows, top_count = expert_ids.shape
    experts = NZ * NY * NC
    cap = 3 * tok_rows * top_count // (2 * experts)
    blocks = NZ * NC
    ff = w_in.shape[2] // 2
    chunk = blocks * cap
    me = lax.axis_index("expert")
    z, y, c = me // (NY * NC), (me // NC) % NY, me % NC
    dp = lax.axis_index("dp")
    zl, x = dp // NX, dp % NX

    def index_of(step):
        return ((zl + step // NX) % NL) * NX + (x + step % NX) % NX

    def take_rows(full, step):
        rows = full.shape[0] // (NL * NX)
        return lax.dynamic_slice_in_dim(full, index_of(step) * rows, rows, 0)

    steps = jnp.arange(NL * NX, dtype=jnp.int32)
    order = index_of(steps)
    steps = jnp.arange(NY, dtype=jnp.int32)
    wanted = z * (NY * NC) + steps * NC + c
    model = tokens.shape[1]

    table = jnp.concatenate([expert_ids.T.astype(BF16), gate_probs.T], axis=0)
    table = jnp.pad(table, ((0, PAD - 2 * top_count), (0, model - tok_rows)))
    rows = jnp.concatenate([tokens, table], axis=0)
    own_in, own_out = w_in[0], w_out[0]
    rows_c = hop(rows, dc=1)

    def gather(weighted, metas, rows):
        outs = [((len(rows) * cap * NY, model), BF16)]
        ins = [wanted, *metas, *rows]
        return call(functools.partial(gather_kernel, weighted, cap), outs, ins, len(metas))[0]

    rows_z = hop(rows, dz=1)
    in_start = after(own_in, rows)
    in_left, in_right = ring(in_start, dx=1), ring(in_start, dx=-1)
    rows_zc = hop(after(rows_z, in_left, in_right), dc=1)
    metas = [rows, rows_c, rows_z, rows_zc]
    tok_rows_out = gather(False, metas, metas)
    tok_part = over_y(tok_rows_out)

    half = own_in.shape[0] // 2
    two_a, two_b = ring(in_left[:half], dx=1), ring(in_right[half:], dx=-1)
    out_far = ring(after(own_out, rows_z), dz=1)
    out_pair = after(jnp.concatenate([own_out, out_far], axis=0), in_left, in_right)
    out_left, out_right = ring(out_pair, dx=1), ring(out_pair, dx=-1)
    oh = own_out.shape[0]
    cot_z = hop(after(cotangent, rows_z), dz=1)
    in_far = ring(after(own_in, out_far), dz=1)
    near_far = after(in_far, two_a, two_b, out_left, out_right)
    in_far_left, in_far_right = ring(near_far, dx=1), ring(near_far, dx=-1)
    in_far_two = ring(after(jnp.concatenate([two_a, two_b], axis=0), in_far), dz=1)
    cot_c = hop(after(cotangent, tok_rows_out), dc=1)
    cot_zc = hop(cot_z, dc=1)
    cots = [cotangent, cot_c, cot_z, cot_zc]
    cots_late = list(lax.optimization_barrier((*cots, two_a, two_b, out_left, out_right))[:4])
    cot_rows = gather(True, metas, cots_late)
    out_grad = over_y(after(cot_rows, in_far))
    parts = [tok_part]
    shards = [
        own_in, in_right, two_a, two_b, in_left, in_far, in_far_right, in_far_two, in_far_left,
    ]
    shards = list(lax.optimization_barrier((*shards, cot_rows))[:9])
    slots = NY * chunk
    pre, full_in, expert_in = call(
        functools.partial(pre_kernel, len(parts)),
        [((slots, 2 * ff), F32), ((model, 2 * ff), BF16), ((slots, model), BF16)],
        [order, *parts, *shards],
        hbm_ins=len(parts) + 9,
        hbm_outs=2,
        scratch=[
            pltpu.VMEM((slots, model), BF16),
            pltpu.VMEM((model, 2 * ff), BF16),
            pltpu.SemaphoreType.DMA((NY * len(parts) + 9,)),
            pltpu.SemaphoreType.DMA((2,)),
        ],
    )
    out_left, out_right = lax.optimization_barrier(
        (out_left, out_right, in_far_left, in_far_right)
    )[:2]
    out_two_a, out_two_b = ring(out_left[:oh], dx=1), ring(out_right[oh:], dx=-1)
    expert_out, hidden, full_out = call(
        out_kernel,
        [((slots, model), BF16), ((slots, ff), BF16), ((ff, model), BF16)],
        [order, pre, own_out, out_far, out_left, out_right, out_two_a, out_two_b],
        hbm_ins=6,
        hbm_outs=1,
        scratch=[
            pltpu.VMEM((ff, model), BF16),
            pltpu.SemaphoreType.DMA((8,)),
            pltpu.SemaphoreType.DMA,
        ],
    )
    layer_rows = over_y(expert_out)
    term_out = dot(hidden, out_grad, ((0,), (0,))).astype(BF16)
    gate_part, up_part = pre[:, :ff], pre[:, ff:]
    sig_part = jax.nn.sigmoid(gate_part)
    activated = gate_part * sig_part

    def combine(weighted, rows, metas, cots):
        count = len(metas)
        outs = [((tok_rows, model), F32)] * (count // 2)
        outs += [((count // 2 * tok_rows, model), BF16)]
        outs += [((2 * top_count, tok_rows), F32)] * (2 if weighted else 0)
        return call(
            functools.partial(combine_kernel, weighted, cap, count),
            outs,
            [wanted, *metas, rows, *cots],
            count,
        )

    def out_pair_of(step):
        return [take_rows(term_out, step), take_rows(term_out, NX + step)]

    two_a, two_b = out_pair_of(2)
    got_a, got_b = ring(two_a, dx=1), ring(two_b, dx=-1)
    one, one_far = out_pair_of(1)
    three, three_far = out_pair_of(3)
    to_right = jnp.concatenate([add(one, got_a).astype(BF16), one_far], axis=0)
    to_left = jnp.concatenate([three, add(three_far, got_b).astype(BF16)], axis=0)

    hidden_grad = dot(after(out_grad, term_out), full_out, ((1,), (1,)))
    slope = sig_part * (1.0 + gate_part * (1.0 - sig_part))
    pre_grad = jnp.concatenate(
        [hidden_grad * up_part * slope, hidden_grad * activated], axis=-1
    ).astype(BF16)
    term_in = dot(after(expert_in, got_a, got_b), pre_grad, ((0,), (0,))).astype(BF16)
    slot_grad = dot(after(pre_grad, term_in), full_in, ((1,), (1,))).astype(BF16)
    part = [take_rows(term_in, step) for step in range(NL * NX)]
    part_a, part_b = after(part[5], got_a, got_b), after(part[7], got_a, got_b)
    far_a, far_b = ring(part_a, dx=1), ring(part_b, dx=-1)
    grad_rows = over_y(after(slot_grad, layer_rows))
    two = add(part[2], ring(part[6], dz=1)).astype(BF16)
    two = after(two, far_a, far_b, layer_rows)
    in_a, in_b = ring(two[:half], dx=1), ring(two[half:], dx=-1)
    far = add(part[4], far_a, far_b).astype(BF16)
    far_back = ring(far, dz=1)
    from_left, from_right = ring(after(to_right, far_a), dx=1), ring(after(to_left, far_b), dx=-1)
    one = jnp.concatenate([add(part[1][:half], in_a).astype(BF16), part[1][half:]], axis=0)
    three = jnp.concatenate([part[3][:half], add(part[3][half:], in_b).astype(BF16)], axis=0)
    mine, mine_z, other, gate_mine, gate_other = combine(True, layer_rows, metas, cots)
    got = hop(other, dc=1)
    back = hop((mine_z + got[tok_rows:].astype(F32)).astype(BF16), dz=1)
    layer_out = add(mine, got[:tok_rows], back).astype(BF16)
    gate_near = gate_mine + hop(gate_other, dc=1)

    one, three = after(one, from_left, from_right), after(three, from_left, from_right)
    one_back, three_back = ring(one, dx=1), ring(three, dx=-1)
    grad_in = add(part[0], one_back, three_back, far_back)[None]

    zero, zero_far = out_pair_of(0)
    out_far_sum = add(zero_far, from_left[oh:], from_right[oh:]).astype(BF16)
    out_back = ring(after(out_far_sum, layer_out), dz=1)
    grad_out = add(zero, from_left[:oh], from_right[:oh], out_back)[None]
    mine, mine_z, other = combine(False, grad_rows, metas, ())
    got = hop(other, dc=1)
    back_sum = (mine_z + got[tok_rows:].astype(F32)).astype(BF16)
    gate_far = hop(after(gate_near[top_count:], got), dz=1)
    gate_grad = (gate_near[:top_count] + gate_far).T.astype(BF16)
    back = hop(after(back_sum, one_back, three_back), dz=1)
    tokens_grad = add(mine, got[:tok_rows], back).astype(BF16)
    mom_in, mom_out = lax.optimization_barrier((mom_in, mom_out, got))[:2]
    w_in_new, mom_in_new = lion_update(w_in, mom_in, grad_in)
    w_out_new, mom_out_new = lion_update(w_out, mom_out, grad_out)
    return (layer_out, tokens_grad, gate_grad, w_in_new, w_out_new, mom_in_new, mom_out_new)


def solution(mesh):
    token = P(("dp", "expert"), None)
    weight = P("expert", "dp", None)
    in_specs = (token, token, token, token, weight, weight, weight, weight)
    out_specs = (token, token, token, weight, weight, weight, weight)
    return jax.shard_map(body, mesh=mesh, in_specs=in_specs, out_specs=out_specs, check_vma=False)
```

```python
import functools

import jax
import jax.numpy as jnp
from jax import lax
from jax.experimental import pallas as pl
from jax.experimental.pallas import tpu as pltpu
from jax.sharding import PartitionSpec as P

beta_one = 0.9
beta_two = 0.99
learn_rate = 0.02
decay_rate = 0.1

NZ, NY, NC = 2, 4, 2
NL, NX = 2, 4
TOP = 4
PAD = 16
F32 = jnp.float32
BF16 = jnp.bfloat16


def hop(value, dz=0, dy=0, dc=0):
    pairs = []
    for i in range(NZ * NY * NC):
        z, y, c = i // (NY * NC), (i // NC) % NY, i % NC
        to = ((z + dz) % NZ) * NY * NC + ((y + dy) % NY) * NC + (c + dc) % NC
        pairs.append((i, to))
    return lax.ppermute(value, "expert", pairs)


def over_y(value):
    groups = [
        [(z * NY + y) * NC + c for y in range(NY)] for z in range(NZ) for c in range(NC)
    ]
    return lax.all_to_all(value, "expert", 0, 0, tiled=True, axis_index_groups=groups)


def ring(value, dx=0, dz=0):
    pairs = []
    for i in range(NL * NX):
        z, x = i // NX, i % NX
        pairs.append((i, ((z + dz) % NL) * NX + (x + dx) % NX))
    return lax.ppermute(value, "dp", pairs)


def after(value, *earlier):
    return lax.optimization_barrier((value, *earlier))[0]


def add(*parts):
    total = parts[0].astype(F32)
    for part in parts[1:]:
        total = total + part.astype(F32)
    return total


def lion_update(weight, moment, grad):
    blend = beta_one * moment + (1.0 - beta_one) * grad
    direction = blend / jnp.sqrt(blend * blend + 1.0)
    wide = weight.astype(F32)
    new_weight = (wide - learn_rate * (direction + decay_rate * wide)).astype(BF16)
    new_moment = beta_two * moment + (1.0 - beta_two) * grad
    return (new_weight, new_moment)


def dot(a, b, dims):
    return lax.dot_general(a, b, (dims, ((), ())), preferred_element_type=F32)


def at_row(row, _):
    return row, 0


def call(kernel, outs, ins, metas=0, hbm_ins=0, hbm_outs=0, scratch=()):
    vmem, stay = pl.BlockSpec(memory_space=pltpu.VMEM), pl.BlockSpec(memory_space=pl.ANY)
    specs = [pl.BlockSpec(memory_space=pltpu.SMEM)]
    for table in ins[1 : 1 + metas]:
        last = table.shape[0] // PAD - 1
        specs.append(pl.BlockSpec((PAD, table.shape[0] - PAD), functools.partial(at_row, last)))
    specs += [vmem] * (len(ins) - 1 - metas - hbm_ins) + [stay] * hbm_ins
    return pl.pallas_call(
        kernel,
        out_shape=[jax.ShapeDtypeStruct(*out) for out in outs],
        grid=(1,) if metas else (),
        in_specs=specs,
        out_specs=[vmem] * (len(outs) - hbm_outs) + [stay] * hbm_outs,
        scratch_shapes=list(scratch),
        compiler_params=pltpu.CompilerParams(vmem_limit_bytes=56 << 20),
    )(*ins)


def place_copies(order, pieces, target, rows, sems, base):
    copies = []
    for i, (ref, first, count, step, within) in enumerate(pieces):
        at = pl.multiple_of(order[step] * rows, rows) + within
        copies.append(
            pltpu.make_async_copy(
                ref.at[pl.ds(first, count)], target.at[pl.ds(at, count)], sems.at[base + i]
            )
        )
    return copies


def pre_kernel(count, order, *refs):
    parts, shards = refs[:count], refs[count : count + 9]
    pre, full, rows_out, rows, weight, sems, out_sems = refs[count + 9 :]
    size = parts[0].shape[0] // NY
    shard = shards[0].shape[0]
    half = shard // 2
    row_copies = [
        pltpu.make_async_copy(
            part.at[pl.ds(i * size, size)],
            rows.at[pl.ds((i * count + j) * size, size)],
            sems.at[i * count + j],
        )
        for i in range(NY)
        for j, part in enumerate(parts)
    ]
    own, right, two_a, two_b, left, far, far_right, far_two, far_left = shards
    near = [
        (own, 0, shard, 0, 0), (right, 0, shard, 1, 0), (two_a, 0, half, 2, 0),
        (two_b, 0, half, 2, half), (left, 0, shard, 3, 0),
    ]
    away = [
        (far, 0, shard, 4, 0), (far_right, 0, shard, 5, 0), (far_two, 0, shard, 6, 0),
        (far_left, 0, shard, 7, 0),
    ]
    near = place_copies(order, near, weight, shard, sems, NY * count)
    away = place_copies(order, away, weight, shard, sems, NY * count + 5)
    for copy in row_copies + near + away:
        copy.start()
    plane = shard * NX
    width = weight.shape[1] // 3

    def product(which, columns):
        at = pl.multiple_of(which * plane, plane)
        return dot(rows[:, pl.ds(at, plane)], weight[pl.ds(at, plane), columns], ((1,), (0,)))

    def tiles(step):
        @pl.loop(0, 3)
        def _(tile):
            step(pl.ds(pl.multiple_of(tile * width, width), width))

    for copy in row_copies + near:
        copy.wait()
    out_rows = pltpu.make_async_copy(rows, rows_out, out_sems.at[0])
    out_rows.start()
    here = order[0] // NX

    def first(columns):
        pre[:, columns] = product(here, columns)

    tiles(first)
    for copy in away:
        copy.wait()
    out_full = pltpu.make_async_copy(weight, full, out_sems.at[1])
    out_full.start()

    def second(columns):
        pre[:, columns] += product(1 - here, columns)

    tiles(second)
    out_rows.wait()
    out_full.wait()


def out_kernel(order, pre, own, far, left, right, two_a, two_b, *refs):
    out, hidden, full, weight, sems, out_sem = refs
    shard = own.shape[0]
    pieces = [
        (own, 0, shard, 0, 0), (right, 0, shard, 1, 0), (two_a, 0, shard, 2, 0),
        (left, 0, shard, 3, 0), (far, 0, shard, 4, 0), (right, shard, shard, 5, 0),
        (two_b, 0, shard, 6, 0), (left, shard, shard, 7, 0),
    ]
    copies = place_copies(order, pieces, weight, shard, sems, 0)
    for copy in copies:
        copy.start()
    ff = hidden.shape[1]
    gate = pre[:, :ff]
    hidden[...] = (gate * jax.nn.sigmoid(gate) * pre[:, ff:]).astype(BF16)
    for copy in copies:
        copy.wait()
    out_full = pltpu.make_async_copy(weight, full, out_sem)
    out_full.start()
    width = weight.shape[1] // 4

    @pl.loop(0, 4)
    def _(tile):
        columns = pl.ds(pl.multiple_of(tile * width, width), width)
        out[:, columns] = dot(hidden[...], weight[:, columns], ((1,), (0,))).astype(BF16)

    out_full.wait()


def routing(wanted, metas):
    top = TOP
    rows = metas[0].shape[1]
    tables = [meta[...].astype(F32) for meta in metas]
    ids = [table[:top] for table in tables]
    gates = [table[top : 2 * top] for table in tables]
    hits = [[block == wanted[step].astype(F32) for step in range(NY)] for block in ids]
    member, weight = [], []
    for block, gate in zip(hits, gates, strict=True):
        for hit in block:
            member.append(jnp.max(jnp.where(hit, 1.0, 0.0), axis=0, keepdims=True))
            weight.append(jnp.sum(jnp.where(hit, gate, 0.0), axis=0, keepdims=True))
    below = lax.broadcasted_iota(jnp.int32, (rows, rows), 0)
    right = lax.broadcasted_iota(jnp.int32, (rows, rows), 1)
    before = jnp.where(below < right, 1.0, 0.0).astype(BF16)
    found = jnp.concatenate(member, axis=0)
    position = dot(found.astype(BF16), before, ((1,), (0,)))
    position = jnp.where(found > 0.5, position, -1.0).astype(jnp.int32)
    return hits, weight, position


def one_hot(position, weight, block, cap):
    rows = position.shape[1]
    slot = lax.broadcasted_iota(jnp.int32, (cap, rows), 0)
    parts = []
    for step in range(NY):
        at = block * NY + step
        value = 1.0 if weight is None else weight[at]
        parts.append(jnp.where(slot == position[at : at + 1], value, 0.0))
    return jnp.concatenate(parts, axis=0)


def gather_kernel(weighted, cap, wanted, *refs):
    count = len(refs) // 2
    metas, rows, out = refs[:count], refs[count : 2 * count], refs[2 * count]
    _, weight, position = routing(wanted, metas)
    for block in range(count):
        pick = one_hot(position, weight if weighted else None, block, cap).astype(BF16)
        got = dot(pick, rows[block][: pick.shape[1]], ((1,), (0,))).astype(BF16)
        for step in range(NY):
            at = (step * count + block) * cap
            out[at : at + cap] = got[step * cap : (step + 1) * cap]


def combine_kernel(weighted, cap, count, wanted, *refs):
    metas, slots, refs = refs[:count], refs[count], refs[count + 1 :]
    hits, weight, position = routing(wanted, metas)
    grads = []
    cots, outs = (refs[:count], refs[count:]) if weighted else ((), refs)
    other = outs[count // 2]
    for block in range(count):
        pick = one_hot(position, weight if weighted else None, block, cap).astype(BF16)
        rows = jnp.concatenate(
            [slots[pl.ds((step * count + block) * cap, cap)] for step in range(NY)],
            axis=0,
        )
        total = dot(pick, rows, ((0,), (0,)))
        side = block // 2
        if block % 2 == 0:
            outs[side][...] = total
        else:
            size = total.shape[0]
            other[side * size : (side + 1) * size] = total.astype(BF16)
        if weighted:
            inner = dot(rows, cots[block][...], ((1,), (1,)))
            inner = jnp.where(one_hot(position, None, block, cap) > 0.5, inner, 0.0)
            grad = 0.0
            for step in range(NY):
                value = jnp.sum(inner[step * cap : (step + 1) * cap], axis=0, keepdims=True)
                grad = grad + jnp.where(hits[block][step], value, 0.0)
            grads.append(grad)
    if weighted:
        outs[3][...] = jnp.concatenate(grads[::2], axis=0)
        outs[4][...] = jnp.concatenate(grads[1::2], axis=0)


def body(tokens, cotangent, expert_ids, gate_probs, w_in, w_out, mom_in, mom_out):
    tok_rows, top_count = expert_ids.shape
    experts = NZ * NY * NC
    cap = 3 * tok_rows * top_count // (2 * experts)
    blocks = NZ * NC
    ff = w_in.shape[2] // 2
    chunk = blocks * cap
    me = lax.axis_index("expert")
    z, y, c = me // (NY * NC), (me // NC) % NY, me % NC
    dp = lax.axis_index("dp")
    zl, x = dp // NX, dp % NX

    def index_of(step):
        return ((zl + step // NX) % NL) * NX + (x + step % NX) % NX

    def take_rows(full, step):
        rows = full.shape[0] // (NL * NX)
        return lax.dynamic_slice_in_dim(full, index_of(step) * rows, rows, 0)

    steps = jnp.arange(NL * NX, dtype=jnp.int32)
    order = index_of(steps)
    steps = jnp.arange(NY, dtype=jnp.int32)
    wanted = z * (NY * NC) + steps * NC + c
    model = tokens.shape[1]

    table = jnp.concatenate([expert_ids.T.astype(BF16), gate_probs.T], axis=0)
    table = jnp.pad(table, ((0, PAD - 2 * top_count), (0, model - tok_rows)))
    rows = jnp.concatenate([tokens, table], axis=0)
    own_in, own_out = w_in[0], w_out[0]
    rows_c = hop(rows, dc=1)

    def gather(weighted, metas, rows):
        outs = [((len(rows) * cap * NY, model), BF16)]
        ins = [wanted, *metas, *rows]
        return call(functools.partial(gather_kernel, weighted, cap), outs, ins, len(metas))[0]

    rows_z = hop(rows, dz=1)
    in_start = after(own_in, rows)
    in_left, in_right = ring(in_start, dx=1), ring(in_start, dx=-1)
    rows_zc = hop(after(rows_z, in_left, in_right), dc=1)
    metas = [rows, rows_c, rows_z, rows_zc]
    tok_rows_out = gather(False, metas, metas)
    tok_part = over_y(tok_rows_out)

    half = own_in.shape[0] // 2
    two_a, two_b = ring(in_left[:half], dx=1), ring(in_right[half:], dx=-1)
    out_far = ring(after(own_out, rows_z), dz=1)
    out_pair = after(jnp.concatenate([own_out, out_far], axis=0), in_left, in_right)
    out_left, out_right = ring(out_pair, dx=1), ring(out_pair, dx=-1)
    oh = own_out.shape[0]
    cot_z = hop(after(cotangent, rows_z), dz=1)
    in_far = ring(after(own_in, out_far), dz=1)
    near_far = after(in_far, two_a, two_b, out_left, out_right)
    in_far_left, in_far_right = ring(near_far, dx=1), ring(near_far, dx=-1)
    in_far_two = ring(after(jnp.concatenate([two_a, two_b], axis=0), in_far), dz=1)
    cot_c = hop(after(cotangent, tok_rows_out), dc=1)
    cot_zc = hop(cot_z, dc=1)
    cots = [cotangent, cot_c, cot_z, cot_zc]
    cots_late = list(lax.optimization_barrier((*cots, two_a, two_b, out_left, out_right))[:4])
    cot_rows = gather(True, metas, cots_late)
    out_grad = over_y(after(cot_rows, in_far))
    parts = [tok_part]
    shards = [
        own_in, in_right, two_a, two_b, in_left, in_far, in_far_right, in_far_two, in_far_left,
    ]
    shards = list(lax.optimization_barrier((*shards, cot_rows))[:9])
    slots = NY * chunk
    pre, full_in, expert_in = call(
        functools.partial(pre_kernel, len(parts)),
        [((slots, 2 * ff), F32), ((model, 2 * ff), BF16), ((slots, model), BF16)],
        [order, *parts, *shards],
        hbm_ins=len(parts) + 9,
        hbm_outs=2,
        scratch=[
            pltpu.VMEM((slots, model), BF16),
            pltpu.VMEM((model, 2 * ff), BF16),
            pltpu.SemaphoreType.DMA((NY * len(parts) + 9,)),
            pltpu.SemaphoreType.DMA((2,)),
        ],
    )
    out_left, out_right = lax.optimization_barrier(
        (out_left, out_right, in_far_left, in_far_right)
    )[:2]
    out_two_a, out_two_b = ring(out_left[:oh], dx=1), ring(out_right[oh:], dx=-1)
    expert_out, hidden, full_out = call(
        out_kernel,
        [((slots, model), BF16), ((slots, ff), BF16), ((ff, model), BF16)],
        [order, pre, own_out, out_far, out_left, out_right, out_two_a, out_two_b],
        hbm_ins=6,
        hbm_outs=1,
        scratch=[
            pltpu.VMEM((ff, model), BF16),
            pltpu.SemaphoreType.DMA((8,)),
            pltpu.SemaphoreType.DMA,
        ],
    )
    layer_rows = over_y(expert_out)
    term_out = dot(hidden, out_grad, ((0,), (0,))).astype(BF16)
    gate_part, up_part = pre[:, :ff], pre[:, ff:]
    sig_part = jax.nn.sigmoid(gate_part)
    activated = gate_part * sig_part

    def combine(weighted, rows, metas, cots):
        count = len(metas)
        outs = [((tok_rows, model), F32)] * (count // 2)
        outs += [((count // 2 * tok_rows, model), BF16)]
        outs += [((2 * top_count, tok_rows), F32)] * (2 if weighted else 0)
        return call(
            functools.partial(combine_kernel, weighted, cap, count),
            outs,
            [wanted, *metas, rows, *cots],
            count,
        )

    def out_pair_of(step):
        return [take_rows(term_out, step), take_rows(term_out, NX + step)]

    two_a, two_b = out_pair_of(2)
    got_a, got_b = ring(two_a, dx=1), ring(two_b, dx=-1)
    one, one_far = out_pair_of(1)
    three, three_far = out_pair_of(3)
    to_right = jnp.concatenate([add(one, got_a).astype(BF16), one_far], axis=0)
    to_left = jnp.concatenate([three, add(three_far, got_b).astype(BF16)], axis=0)

    hidden_grad = dot(after(out_grad, term_out), full_out, ((1,), (1,)))
    slope = sig_part * (1.0 + gate_part * (1.0 - sig_part))
    pre_grad = jnp.concatenate(
        [hidden_grad * up_part * slope, hidden_grad * activated], axis=-1
    ).astype(BF16)
    term_in = dot(after(expert_in, got_a, got_b), pre_grad, ((0,), (0,))).astype(BF16)
    slot_grad = dot(after(pre_grad, term_in), full_in, ((1,), (1,))).astype(BF16)
    part = [take_rows(term_in, step) for step in range(NL * NX)]
    part_a, part_b = after(part[5], got_a, got_b), after(part[7], got_a, got_b)
    far_a, far_b = ring(part_a, dx=1), ring(part_b, dx=-1)
    grad_rows = over_y(after(slot_grad, layer_rows))
    two = add(part[2], ring(part[6], dz=1)).astype(BF16)
    two = after(two, far_a, far_b, layer_rows)
    in_a, in_b = ring(two[:half], dx=1), ring(two[half:], dx=-1)
    far = add(part[4], far_a, far_b).astype(BF16)
    far_back = ring(far, dz=1)
    from_left, from_right = ring(after(to_right, far_a), dx=1), ring(after(to_left, far_b), dx=-1)
    one = jnp.concatenate([add(part[1][:half], in_a).astype(BF16), part[1][half:]], axis=0)
    three = jnp.concatenate([part[3][:half], add(part[3][half:], in_b).astype(BF16)], axis=0)
    mine, mine_z, other, gate_mine, gate_other = combine(True, layer_rows, metas, cots)
    got = hop(other, dc=1)
    back = hop((mine_z + got[tok_rows:].astype(F32)).astype(BF16), dz=1)
    layer_out = add(mine, got[:tok_rows], back).astype(BF16)
    gate_near = gate_mine + hop(gate_other, dc=1)

    one, three = after(one, from_left, from_right), after(three, from_left, from_right)
    one_back, three_back = ring(one, dx=1), ring(three, dx=-1)
    grad_in = add(part[0], one_back, three_back, far_back)[None]

    zero, zero_far = out_pair_of(0)
    out_far_sum = add(zero_far, from_left[oh:], from_right[oh:]).astype(BF16)
    out_back = ring(after(out_far_sum, layer_out), dz=1)
    grad_out = add(zero, from_left[:oh], from_right[:oh], out_back)[None]
    mine, mine_z, other = combine(False, grad_rows, metas, ())
    got = hop(other, dc=1)
    back_sum = (mine_z + got[tok_rows:].astype(F32)).astype(BF16)
    gate_far = hop(after(gate_near[top_count:], got), dz=1)
    gate_grad = (gate_near[:top_count] + gate_far).T.astype(BF16)
    back = hop(after(back_sum, one_back, three_back), dz=1)
    tokens_grad = add(mine, got[:tok_rows], back).astype(BF16)
    mom_in, mom_out = lax.optimization_barrier((mom_in, mom_out, got))[:2]
    w_in_new, mom_in_new = lion_update(w_in, mom_in, grad_in)
    w_out_new, mom_out_new = lion_update(w_out, mom_out, grad_out)
    return (layer_out, tokens_grad, gate_grad, w_in_new, w_out_new, mom_in_new, mom_out_new)


def solution(mesh):
    token = P(("dp", "expert"), None)
    weight = P("expert", "dp", None)
    in_specs = (token, token, token, token, weight, weight, weight, weight)
    out_specs = (token, token, token, weight, weight, weight, weight)
    return jax.shard_map(body, mesh=mesh, in_specs=in_specs, out_specs=out_specs, check_vma=False)
```
